32 devices in a mesh: stn: 2 (over x), tm: 16 (over z, y, core).
Axes of the slice: x: 2, y: 2, z: 4, core: 2. Of those that a mesh axis runs over, the one named last changes fastest.
Arguments:
- spectra: bfloat16 [16, 8, 64, 2, 4096], P('stn', None, 'tm'), may hold values from -6 to 6
- flags: int32 [16, 8, 64, 32], P('stn', None, 'tm'), may hold values from 0 to 1, as said below
- poly_index: int32 [16, 8, 64], P('stn', None, 'tm'), may hold values from 0 to 63
- delay_model: float32 [64, 3], replicated, may hold values from -48 to 48
- partner_order: int32 [16], replicated, may hold values from 0 to 15, each once
Outputs:
- fringe: float32 [2, 256, 8, 256], P(None, ('stn', 'tm'))
The draws below stay inside these ranges and needn't reach their ends.
Inputs may be any that keep to these rules, and one draw needn't show every extreme that they name: `flags`: 1 marks a flagged block; whole blocks of a station can be flagged for the full window. `partner_order`: each station appears once.
All inputs are finite; a program needn't handle non-finite values.
Results may differ from the reference program's by a relative error of at most 0.003.
Values may be sent and summed in bfloat16 or wider, within the bound.
A program may use at most 128 MiB of HBM per device.

```python
import math
import jax
import jax.numpy as jnp
from jax import lax

S = 16
C = 4096
P_SIZE = 8
LAGS = 256
NPOLY = 64
SPP = 64
CB = 32


def model_rows(key):
    sign_key = jax.random.fold_in(key, 11)
    size_key = jax.random.fold_in(key, 12)
    mixed_key = jax.random.fold_in(key, 13)
    pick_key = jax.random.fold_in(key, 14)
    signs = jnp.where(jax.random.randint(sign_key, (NPOLY, 1), 0, 2) == 0, -1.0, 1.0).astype(jnp.float32)
    aligned = signs * jax.random.uniform(size_key, (NPOLY, 3), jnp.float32, 16.0, 48.0)
    mixed = jax.random.uniform(mixed_key, (NPOLY, 3), jnp.float32, -48.0, 48.0)
    picked = jax.random.randint(pick_key, (NPOLY, 1), 0, 4) == 0
    return jnp.where(picked, mixed, aligned)


def index_rows(key):
    return jax.random.randint(jax.random.fold_in(key, 21), (S, P_SIZE, SPP), 0, NPOLY).astype(jnp.int32)


def draw_delay_model(key, part):
    return model_rows(key)


def draw_poly_index(key, part):
    return index_rows(key)


def draw_spectra(key, part):
    model = model_rows(key)
    index = index_rows(key)
    coeffs = model[index]
    times = (jnp.arange(P_SIZE, dtype=jnp.int32)[:, None] * SPP + jnp.arange(SPP, dtype=jnp.int32)[None, :]).astype(jnp.float32)
    moment = times / float(P_SIZE * SPP)
    delay = coeffs[..., 0] + coeffs[..., 1] * moment + coeffs[..., 2] * moment * moment
    common = jnp.clip(jax.random.normal(jax.random.fold_in(key, 31), (2, P_SIZE, SPP, C), jnp.float32), -4.5, 4.5)
    offsets = jax.random.randint(jax.random.fold_in(key, 41), (S,), -(C // 6), C // 6 + 1).astype(jnp.int32)
    channel = jnp.arange(C, dtype=jnp.int32)
    freq = channel.astype(jnp.float32) * (math.pi / C)
    gains = jnp.ones((S,), jnp.float32)
    strength = 0.5
    noise_base = jax.random.fold_in(key, 51)

    def one_station(items):
        station, station_delay, offset, gain = items
        noise_key = jax.random.fold_in(noise_base, station)
        noise = jnp.clip(jax.random.normal(noise_key, (P_SIZE, SPP, 2, C), jnp.float32), -4.5, 4.5)
        turns = channel * offset % C
        angle = station_delay[..., None] * freq - turns.astype(jnp.float32) * (2.0 * math.pi / C)
        cosine = jnp.cos(angle)
        sine = jnp.sin(angle)
        real = strength * (common[0] * cosine - common[1] * sine)
        imag = strength * (common[0] * sine + common[1] * cosine)
        signal = jnp.stack([real, imag], axis=2)
        return jnp.clip(gain * noise + signal, -6.0, 6.0)
    stations = lax.map(one_station, (jnp.arange(S, dtype=jnp.int32), delay, offsets, gains))
    return stations.astype(jnp.bfloat16)


def draw_flags(key, part):
    sample_key = jax.random.fold_in(key, 101)
    whole_key = jax.random.fold_in(key, 202)
    shared_key = jax.random.fold_in(key, 303)
    sample = jax.random.randint(sample_key, (S, P_SIZE, SPP, CB), 0, 8) == 0
    whole = jax.random.randint(whole_key, (S, 1, 1, CB), 0, 16) == 0
    shared = jax.random.randint(shared_key, (1, P_SIZE, SPP, CB), 0, 3) == 0
    return jnp.logical_or(jnp.logical_or(sample, whole), shared).astype(jnp.int32)


def setup_inputs(seed: int = 0) -> dict:
    key_of = jax.random.split(jax.random.key(seed), 6)
    return {
        "spectra": draw_spectra(jax.random.fold_in(key_of[5], 71), 0),
        "flags": draw_flags(jax.random.fold_in(key_of[5], 71), 0),
        "poly_index": draw_poly_index(jax.random.fold_in(key_of[5], 71), 0),
        "delay_model": draw_delay_model(jax.random.fold_in(key_of[5], 71), 0),
        "partner_order": jax.random.permutation(key_of[4], S).astype(jnp.int32),
    }


def rotate(spectra, flags, coeffs, times, total_time):
    channels = spectra.shape[-1]
    blocks = flags.shape[-1]
    moment = times / total_time
    delay = coeffs[..., 0] + coeffs[..., 1] * moment + coeffs[..., 2] * moment * moment
    freq = jnp.arange(channels, dtype=jnp.int32).astype(jnp.float32) * (math.pi / channels)
    phase = delay[..., None] * freq
    cosine = jnp.cos(phase)
    sine = jnp.sin(phase)
    real = spectra[..., 0, :].astype(jnp.float32)
    imag = spectra[..., 1, :].astype(jnp.float32)
    weight = 1.0 - flags.astype(jnp.float32)
    weight = jnp.broadcast_to(weight[..., None], weight.shape + (channels // blocks,)).reshape(real.shape)
    new_real = weight * (real * cosine + imag * sine)
    new_imag = weight * (imag * cosine - real * sine)
    return jnp.stack([new_real, new_imag], axis=-2).astype(jnp.bfloat16)

def transform(vis, counts, lags):
    rows, periods, _, channels = vis.shape
    blocks = counts.shape[-1]
    scale = 1.0 / jnp.sqrt(jnp.maximum(counts, 1.0))
    normed = vis.reshape(rows, periods, 2, blocks, channels // blocks) * scale[:, :, None, :, None]
    normed = normed.reshape(rows, periods, 2, channels)
    index = jnp.arange(lags, dtype=jnp.int32)
    middle = lags // 2
    delays = jnp.where(index < middle, index - middle, index - middle + 1)
    turns = jnp.arange(channels, dtype=jnp.int32)[:, None] * delays[None, :] % channels
    angle = turns.astype(jnp.float32) * (2.0 * math.pi / channels)
    cosine = jnp.cos(angle)
    sine = jnp.sin(angle)
    highest = lax.Precision.HIGHEST
    real = normed[:, :, 0].reshape(rows * periods, channels)
    imag = normed[:, :, 1].reshape(rows * periods, channels)
    part_real = jnp.dot(real, cosine, precision=highest) + jnp.dot(imag, sine, precision=highest)
    part_imag = jnp.dot(imag, cosine, precision=highest) - jnp.dot(real, sine, precision=highest)
    part_real = part_real.reshape(rows, periods, lags)
    part_imag = part_imag.reshape(rows, periods, lags)
    pidx = jnp.arange(periods, dtype=jnp.int32)
    pturn = pidx[:, None] * pidx[None, :] % periods
    pangle = pturn.astype(jnp.float32) * (2.0 * math.pi / periods)
    pcos = jnp.cos(pangle)
    psin = jnp.sin(pangle)
    out_real = jnp.einsum('rp,npl->nrl', pcos, part_real, precision=highest) + jnp.einsum('rp,npl->nrl', psin, part_imag, precision=highest)
    out_imag = jnp.einsum('rp,npl->nrl', pcos, part_imag, precision=highest) - jnp.einsum('rp,npl->nrl', psin, part_real, precision=highest)
    factor = 1.0 / math.sqrt(periods * channels)
    return jnp.stack([out_real, out_imag]) * factor

def reference(spectra, flags, poly_index, delay_model, partner_order):
    stations, periods, depth, _, channels = spectra.shape
    times = (jnp.arange(periods, dtype=jnp.int32)[:, None] * depth + jnp.arange(depth, dtype=jnp.int32)[None, :]).astype(jnp.float32)
    total_time = float(periods * depth)

    def one_station(items):
        spectrum, flag, index = items
        coeffs = delay_model[index]
        return rotate(spectrum[None], flag[None], coeffs[None], times, total_time)[0]
    rotated = lax.map(one_station, (spectra, flags, poly_index))
    wide = rotated.astype(jnp.float32)

    def one_row(mine):
        product = jnp.einsum('pkxc,bpkyc->bpxyc', mine.astype(jnp.float32), wide)
        real = product[:, :, 0, 0] + product[:, :, 1, 1]
        imag = product[:, :, 1, 0] - product[:, :, 0, 1]
        return jnp.stack([real, imag], axis=2)
    vis = lax.map(one_row, rotated)
    weight = 1.0 - flags.astype(jnp.float32)
    counts = jnp.einsum('apkx,bpkx->abpx', weight, weight, precision=lax.Precision.HIGHEST)
    vis = jnp.take(vis, partner_order, axis=1).reshape(stations * stations, periods, 2, channels)
    counts = jnp.take(counts, partner_order, axis=1).reshape(stations * stations, periods, counts.shape[-1])
    return transform(vis, counts, LAGS)
```

```python
import functools
import math

import jax
import jax.numpy as jnp
import numpy as np
from jax import lax
from jax.experimental import pallas as pl
from jax.experimental.pallas import tpu as pltpu
from jax.sharding import PartitionSpec as P

LAGS = 256
QUARTERS = 4
LANES = 128


def lag_tables(channels):
    lags = np.arange(1, LAGS // 2 + 1)
    j = np.arange(channels // QUARTERS)
    angle = (j[:, None] * lags[None, :] % channels) * (2.0 * np.pi / channels)
    table = np.concatenate([np.cos(angle), np.sin(angle)], axis=1).astype(np.float32)
    high = table.astype(jnp.bfloat16)
    low = (table - high.astype(np.float32)).astype(jnp.bfloat16)
    return high, low


def split(value):
    high = value.astype(jnp.bfloat16)
    low = (value - high.astype(jnp.float32)).astype(jnp.bfloat16)
    return high, low


def dot(a, b):
    return jnp.dot(a, b, preferred_element_type=jnp.float32)


def correlate_kernel(x_ref, e1_ref, e2_ref, scale_ref, wh_ref, wl_ref, pick_ref, out_ref, y_ref, vh_ref, vl_ref, z_ref):
    depth, _, stations, width = x_ref.shape[1:]
    half = stations // 2
    blocks = width // LANES
    quarter = pl.program_id(1)

    def put(row, col, value):
        high, low = split(value)
        cols = slice(col * LANES, (col + 1) * LANES)
        vh_ref[row : row + stations, cols] = high
        vl_ref[row : row + stations, cols] = low

    for h in range(blocks):
        cols = slice(h * LANES, (h + 1) * LANES)
        slot = h % 2
        mine = []
        for k in range(depth):
            c1 = e1_ref[0, 0, k, 0, :, h : h + 1]
            s1 = e1_ref[0, 0, k, 1, :, h : h + 1]
            c2 = e2_ref[0, k, 0]
            s2 = e2_ref[0, k, 1]
            cosine = c1 * c2 - s1 * s2
            sine = s1 * c2 + c1 * s2
            real = x_ref[0, k, 0, :, cols].astype(jnp.float32)
            imag = x_ref[0, k, 1, :, cols].astype(jnp.float32)
            new_real = (real * cosine + imag * sine).astype(jnp.bfloat16).astype(jnp.float32)
            new_imag = (imag * cosine - real * sine).astype(jnp.bfloat16).astype(jnp.float32)
            y_ref[slot, k, 0, :stations] = new_real
            y_ref[slot, k, 1, :stations] = new_imag
            y_ref[slot, k, 0, stations:] = new_real[:half]
            y_ref[slot, k, 1, stations:] = new_imag[:half]
            mine.append((new_real, new_imag))
        for d in range(half + 1):
            count = half if d == half else stations
            real = None
            imag = None
            for k in range(depth):
                ar, ai = mine[k]
                ar, ai = ar[:count], ai[:count]
                if d == 0:
                    br, bi = ar, ai
                else:
                    br = y_ref[slot, k, 0, d : d + count]
                    bi = y_ref[slot, k, 1, d : d + count]
                term = ar * br + ai * bi
                real = term if real is None else real + term
                if d > 0:
                    term = ai * br - ar * bi
                    imag = term if imag is None else imag + term
            scale = scale_ref[0, 0, d * stations : d * stations + count, h : h + 1]
            if d == half:
                both = jnp.concatenate([real * scale, imag * scale], axis=0)
                put(stations * (stations - 1), h, both)
            else:
                put(d * stations, h, real * scale)
                if d > 0:
                    put((half + d - 1) * stations, h, imag * scale)

    vh = vh_ref[...]
    part = dot(vh, wh_ref[...]) + dot(vh, wl_ref[...]) + dot(vl_ref[...], wh_ref[...])
    lags = part.shape[1] // 2
    part_c = part[:, :lags]
    part_s = part[:, lags:]
    lag = lax.broadcasted_iota(jnp.int32, part_c.shape, 1) + 1
    turn = (lag * quarter) % 4
    cq = jnp.where(turn == 0, 1.0, jnp.where(turn == 2, -1.0, 0.0))
    sq = jnp.where(turn == 1, 1.0, jnp.where(turn == 3, -1.0, 0.0))
    new_c = part_c * cq - part_s * sq
    new_s = part_s * cq + part_c * sq

    @pl.when(quarter == 0)
    def _():
        z_ref[:, :lags] = new_c
        z_ref[:, lags:] = new_s

    @pl.when(quarter > 0)
    def _():
        z_ref[:, :lags] += new_c
        z_ref[:, lags:] += new_s

    @pl.when(quarter == QUARTERS - 1)
    def _():
        z = z_ref[...]
        high = z.astype(jnp.bfloat16)
        rest = z - high.astype(jnp.float32)
        mid, low = split(rest)
        pick = pick_ref[...]
        rows = dot(pick, high) + dot(pick, mid) + dot(pick, low)
        out_ref[...] = rows.reshape(out_ref.shape)


def correlate(x, e1, e2, scale, high, low, pick, owners):
    periods, depth, _, stations, channels = x.shape
    width = channels // QUARTERS
    rows = stations * stations
    return pl.pallas_call(
        correlate_kernel,
        grid=(periods, QUARTERS),
        in_specs=[
            pl.BlockSpec((1, depth, 2, stations, width), lambda p, q: (p, 0, 0, 0, q)),
            pl.BlockSpec((1, 1) + e1.shape[2:], lambda p, q: (p, q, 0, 0, 0, 0)),
            pl.BlockSpec((1,) + e2.shape[1:], lambda p, q: (p, 0, 0, 0, 0)),
            pl.BlockSpec((1, 1) + scale.shape[2:], lambda p, q: (p, q, 0, 0)),
            pl.BlockSpec(high.shape, lambda p, q: (0, 0)),
            pl.BlockSpec(low.shape, lambda p, q: (0, 0)),
            pl.BlockSpec(pick.shape, lambda p, q: (0, 0)),
        ],
        out_specs=pl.BlockSpec((owners, 1, 2 * rows // owners, LAGS), lambda p, q: (0, p, 0, 0)),
        out_shape=jax.ShapeDtypeStruct((owners, periods, 2 * rows // owners, LAGS), jnp.float32),
        scratch_shapes=[
            pltpu.VMEM((2, depth, 2, stations + stations // 2, LANES), jnp.float32),
            pltpu.VMEM((rows, width), jnp.bfloat16),
            pltpu.VMEM((rows, width), jnp.bfloat16),
            pltpu.VMEM((rows, LAGS), jnp.float32),
        ],
        compiler_params=pltpu.CompilerParams(dimension_semantics=("arbitrary", "arbitrary")),
        name="correlate",
    )(x, e1, e2, scale, high, low, pick)


def finish_kernel(factor, g_ref, pc_ref, ps_ref, out_ref):
    highest = lax.Precision.HIGHEST
    lags = g_ref.shape[-1] // 2
    rc, rs = g_ref[0, :, :lags], g_ref[0, :, lags:]
    ic, im_s = g_ref[1, :, :lags], g_ref[1, :, lags:]
    flip = (
        lax.broadcasted_iota(jnp.int32, (lags, lags), 0) + lax.broadcasted_iota(jnp.int32, (lags, lags), 1) == lags - 1
    ).astype(jnp.float32)
    pcos = pc_ref[...]
    psin = ps_ref[...]

    def mix(m, v):
        return jnp.dot(m, v, precision=highest, preferred_element_type=jnp.float32)

    for side in range(2):
        if side == 0:
            real, imag = mix(rc - im_s, flip), mix(ic + rs, flip)
        else:
            real, imag = rc + im_s, ic - rs
        cols = slice(side * lags, (side + 1) * lags)
        out_ref[0, :, cols] = (mix(pcos, real) + mix(psin, imag)) * factor
        out_ref[1, :, cols] = (mix(pcos, imag) - mix(psin, real)) * factor


def finish(g, periods, channels):
    rows = g.shape[1] // periods
    idx = np.arange(periods)
    angle = (idx[:, None] * idx[None, :] % periods) * (2.0 * np.pi / periods)
    eye = np.eye(rows)

    def table(m):
        wide = np.einsum("rp,nm->nrpm", m, eye).reshape(rows * periods, periods * rows)
        return jnp.asarray(wide.astype(np.float32))

    out = pl.pallas_call(
        functools.partial(finish_kernel, 1.0 / math.sqrt(periods * channels)),
        out_shape=jax.ShapeDtypeStruct((2, rows * periods, LAGS), jnp.float32),
        name="finish",
    )(g, table(np.cos(angle)), table(np.sin(angle)))
    return out.reshape(2, rows, periods, LAGS)


def pick_matrix(partner_order, stations, first_station, groups, owners):
    half = stations // 2
    own_rows = stations * stations // (groups * owners)
    n = np.arange(stations * stations).reshape(groups, owners, own_rows).transpose(1, 0, 2)
    a = jnp.asarray(n // stations, jnp.int32)
    onehot = (jnp.asarray(n % stations, jnp.int32)[..., None] == jnp.arange(stations)).astype(jnp.int32)
    b = jnp.sum(onehot * partner_order, axis=-1)
    a = (a - first_station) % stations
    b = (b - first_station) % stations
    d = (b - a) % stations
    flip = (d > half) | ((d == half) & (a >= half))
    d = jnp.where(flip, (stations - d) % stations, d)
    row = jnp.where(flip, b, a)
    top = stations * (stations - 1)
    real_col = jnp.where(d == half, top + row, d * stations + row)
    imag_col = jnp.where(d == half, top + half + row, (half + d - 1) * stations + row)
    imag_col = jnp.where(d == 0, -1, imag_col)
    sign = jnp.where(flip, -1.0, 1.0)
    col = jnp.stack([real_col, imag_col], axis=2)
    value = jnp.stack([jnp.ones_like(sign), sign], axis=2)
    pick = jnp.where(col[..., None] == jnp.arange(stations * stations), value[..., None], 0.0)
    return pick.reshape(2 * stations * stations, stations * stations).astype(jnp.bfloat16)


def per_device(spectra, flags, poly_index, delay_model, partner_order):
    local, periods, depth, _, channels = spectra.shape
    groups = lax.axis_size("stn")
    owners = lax.axis_size("tm")
    me = lax.axis_index("stn")
    stations = local * groups
    mine = periods // groups
    blocks = flags.shape[-1]
    first_station = (me + 1) % groups * local

    chunks = []
    for i in range(mine):
        pieces = []
        for shift in range(groups - 1, -1, -1):
            target = (me + shift) % groups
            piece = lax.dynamic_slice_in_dim(spectra, target * mine + i, 1, axis=1)
            if shift:
                piece = lax.ppermute(piece, "stn", [(g, (g + shift) % groups) for g in range(groups)])
            pieces.append(piece)
        chunks.append(jnp.concatenate(pieces, axis=0).transpose(1, 2, 3, 0, 4))

    ints = jnp.concatenate([flags, poly_index[..., None]], axis=-1)
    ints = lax.all_to_all(ints, "stn", split_axis=1, concat_axis=0, tiled=True)
    ints = jnp.roll(ints, -first_station, axis=0)
    weight = 1.0 - ints[..., :blocks].astype(jnp.float32)
    index = ints[..., blocks]

    pairs = jnp.stack([weight * jnp.roll(weight, -d, axis=0) for d in range(stations // 2 + 1)])
    counts = jnp.sum(pairs, axis=3).reshape((stations // 2 + 1) * stations, mine, blocks)
    counts = lax.psum(counts.astype(jnp.bfloat16), "tm").astype(jnp.float32)
    scale = 1.0 / jnp.sqrt(jnp.maximum(counts, 1.0))
    scale = scale.reshape(scale.shape[0], mine, QUARTERS, blocks // QUARTERS).transpose(1, 2, 0, 3)

    total = depth * owners
    times = (
        (me * mine + jnp.arange(mine, dtype=jnp.int32))[:, None] * total
        + lax.axis_index("tm") * depth
        + jnp.arange(depth, dtype=jnp.int32)[None, :]
    ).astype(jnp.float32)
    moment = times / float(periods * total)
    table_rows = delay_model.shape[0]
    onehot = (index[..., None] == jnp.arange(table_rows, dtype=jnp.int32)).astype(jnp.float32)
    coeffs = jnp.dot(onehot.reshape(-1, table_rows), delay_model, precision=lax.Precision.HIGHEST)
    coeffs = coeffs.reshape(stations, mine, depth, 3)
    delay = coeffs[..., 0] + coeffs[..., 1] * moment + coeffs[..., 2] * moment * moment
    step = math.pi / channels
    coarse = delay[..., None] * (jnp.arange(blocks, dtype=jnp.int32).astype(jnp.float32) * (step * (channels // blocks)))
    fine = delay[..., None] * (jnp.arange(channels // blocks, dtype=jnp.int32).astype(jnp.float32) * step)
    e1 = jnp.stack([weight * jnp.cos(coarse), weight * jnp.sin(coarse)], axis=3)
    e1 = e1.reshape(stations, mine, depth, 2, QUARTERS, blocks // QUARTERS).transpose(1, 4, 2, 3, 0, 5)
    e2 = jnp.stack([jnp.cos(fine), jnp.sin(fine)], axis=3).transpose(1, 2, 3, 0, 4)

    high, low = lag_tables(channels)
    high, low = jnp.asarray(high), jnp.asarray(low)
    pick = pick_matrix(partner_order, stations, first_station, groups, owners)
    done = []
    for i in range(mine):
        part = correlate(chunks[i], e1[i : i + 1], e2[i : i + 1], scale[i : i + 1], high, low, pick, owners)
        done.append(lax.psum_scatter(part, "tm", scatter_dimension=0, tiled=True)[0])
    own = jnp.concatenate(done, axis=0)
    own = own.reshape(mine, groups, 2, -1, LAGS)
    own = lax.all_to_all(own, "stn", split_axis=1, concat_axis=0, tiled=True)
    own = own.reshape(periods, 2, -1, LAGS).transpose(1, 0, 2, 3).reshape(2, -1, LAGS)
    return finish(own, periods, channels)


def solution(mesh):
    return jax.shard_map(
        per_device,
        mesh=mesh,
        in_specs=(
            P("stn", None, "tm", None, None),
            P("stn", None, "tm", None),
            P("stn", None, "tm"),
            P(),
            P(),
        ),
        out_specs=P(None, ("stn", "tm"), None, None),
        check_vma=False,
    )
```
